256 devices in a mesh: slab: 4 (over x), panel: 64 (over z, y, core).
Axes of the slice: x: 4, y: 4, z: 8, core: 2. Of those that a mesh axis runs over, the one named last changes fastest.
Arguments:
- trial: bfloat16 [1600, 6400], P('slab', 'panel'), may hold values from -6 to 6
- integrals: bfloat16 [6400, 256, 300], P(None, 'panel'), may hold values from -0.078125 to 0.078125
- basis: bfloat16 [2, 1600, 256, 300], P(None, 'slab', 'panel'), may hold values from -0.00048828125 to 0.00048828125
- images: bfloat16 [2, 1600, 256, 300], P(None, 'slab', 'panel'), may hold values from -6 to 6
- current: bfloat16 [1600, 256, 300], P('slab', 'panel'), may hold values from -18 to 18
- occ_energy: float32 [40], replicated, may hold values from -1 to -0.3
- vir_energy: float32 [300], replicated, may hold values from 0.1 to 2
- shift: float32 [1], replicated, may hold values from 0.5 to 1.5
Outputs:
- sigma: bfloat16 [1600, 256, 300], P('slab', 'panel')
- update: bfloat16 [1600, 256, 300], P('slab', 'panel')
- correlations: float32 [2], replicated
The draws below stay inside these ranges and needn't reach their ends.
All inputs are finite; a program needn't handle non-finite values.
Results may differ from the reference program's by a relative error of at most 0.0079.
Values may be sent and summed in bfloat16 or wider, within the bound.
No kernel may reach another device: no remote copies, remote signals or barrier semaphores. Data moves between devices by JAX's collectives and lax.ppermute only.
A program may use at most 128 MiB of HBM per device.

```python
import jax
import jax.numpy as jnp
from jax import lax

OCCUPIED = 40
VIRTUAL = 300
WINDOW = 256
SUBSPACE = 2
PAIRS = 1600
COLUMNS = 6400


def draw_current(key, part):
    shape = (PAIRS, WINDOW, VIRTUAL)
    base = jnp.clip(jax.random.normal(key, shape, jnp.float32), -5.0, 5.0)
    row_scale = 0.5 + 1.5 * jnp.arange(PAIRS, dtype=jnp.float32) / PAIRS
    col_scale = 0.6 + 1.2 * jnp.arange(WINDOW, dtype=jnp.float32) / WINDOW
    return (base * row_scale[:, None, None] * col_scale[None, :, None]).astype(jnp.bfloat16)


def levels(own_key, extent, split, low, largest):
    level = 1.0
    for dim, shards_of in split:
        steps = jax.random.uniform(jax.random.fold_in(jax.random.fold_in(own_key, 6), dim), (shards_of,), jnp.float32, low / len(split), largest / len(split))
        level = level * jnp.repeat(jnp.exp(steps), extent[dim] // shards_of).reshape((-1,) + (1,) * (len(extent) - 1 - dim))
    return level


def noise(key, dims, spread, reach, pieces=(), kind=jnp.bfloat16):
    level = levels(key, dims, pieces, -0.22, 0.18) if pieces else 1.0
    array = jax.random.normal(key, dims, jnp.float32) * spread * level
    return jnp.minimum(jnp.maximum(array, -reach), reach).astype(kind)


def setup_inputs(seed: int = 0) -> dict:
    arg_keys = jax.random.split(jax.random.key(seed), 9)
    return {
        "trial": noise(arg_keys[0], (PAIRS, COLUMNS), 1.0, 6.0, ((0, 4), (1, 64))),
        "integrals": noise(arg_keys[1], (COLUMNS, WINDOW, VIRTUAL), COLUMNS ** -0.5, 0.078125, ((1, 64),)),
        "basis": noise(arg_keys[2], (SUBSPACE, PAIRS, WINDOW, VIRTUAL), (PAIRS * WINDOW * VIRTUAL) ** -0.5, 0.00048828125, ((1, 4), (2, 64))),
        "images": noise(arg_keys[3], (SUBSPACE, PAIRS, WINDOW, VIRTUAL), 1.0, 6.0, ((1, 4), (2, 64))),
        "current": draw_current(jax.random.fold_in(arg_keys[8], 71), 0),
        "occ_energy": jnp.clip(jax.random.uniform(arg_keys[5], (OCCUPIED,), jnp.float32, -1.0, -0.3), -1.0, -0.3),
        "vir_energy": jnp.clip(jax.random.uniform(arg_keys[6], (VIRTUAL,), jnp.float32, 0.1, 2.0), 0.1, 2.0),
        "shift": jnp.clip(jax.random.uniform(arg_keys[7], (1,), jnp.float32, 0.5, 1.5), 0.5, 1.5),
    }


def reference(trial, integrals, basis, images, current, occ_energy, vir_energy, shift):
    flat = integrals.reshape(COLUMNS, WINDOW * VIRTUAL).astype(jnp.float32)
    summed = jnp.dot(trial.astype(jnp.float32), flat, precision=lax.Precision.HIGHEST)
    sigma = summed.astype(jnp.bfloat16).reshape(PAIRS, WINDOW, VIRTUAL)
    sig_full = sigma.astype(jnp.float32)
    correlations = lax.optimization_barrier(jnp.sum(basis.astype(jnp.float32) * sig_full[None], axis=(1, 2, 3)))
    pair_energy = (occ_energy[:, None] + occ_energy[None, :]).reshape(PAIRS)
    energy_b = vir_energy[:WINDOW]
    denom = jnp.maximum(vir_energy[None, None, :] + energy_b[None, :, None] - pair_energy[:, None, None] - shift[0], 1.0)
    resid = sig_full - shift[0] * current.astype(jnp.float32)
    for index in range(SUBSPACE):
        resid = resid - correlations[index] * images[index].astype(jnp.float32)
    delta = resid / denom
    size_sq = jnp.sum(delta * delta)
    update = (delta / jnp.sqrt(size_sq + 1e-06)).astype(jnp.bfloat16)
    return (sigma, update, correlations)
```

```python
import functools

import jax
import jax.numpy as jnp
from jax import lax
from jax.experimental import pallas as pl
from jax.experimental.pallas import tpu as pltpu
from jax.sharding import Mesh, PartitionSpec as P

OCCUPIED = 40
LANES = 128
ROWS = 400
HALF = 200
OWN = 100
SPAN = 800
TILES = 7
WIDE = TILES * LANES
CUT = 512
B = 4
A = 300
APAD = 384
K = 6400
DEVICES = 256
GROUPS = (((0, 0),), ((1, 0), (0, 1)), ((2, 0), (0, 2)), ((3, 0), (0, 3)), ((4, 0),))


VMEM = pl.BlockSpec(memory_space=pltpu.VMEM)
SMEM = pl.BlockSpec(memory_space=pltpu.SMEM)
ANY = pl.BlockSpec(memory_space=pl.ANY)


def params(mib):
    return pltpu.CompilerParams(vmem_limit_bytes=mib << 20)


def near(array):
    return pltpu.with_memory_space_constraint(array, pltpu.VMEM)


def lay_kernel(at, *refs):
    pieces, low, high = refs[:4], refs[4], refs[5]
    z, y, c = at[0], at[1], at[2]
    start = lax.rem(z * SPAN, LANES)
    lane = lax.broadcasted_iota(jnp.int32, (OWN, WIDE), 1)
    row = lax.broadcasted_iota(jnp.int32, (OWN, WIDE), 0)
    gap = lane - row - start
    total = jnp.zeros((HALF, WIDE), jnp.float32)
    for dy in range(4):
        for dc in range(2):
            core = c if dc == 0 else 1 - c
            slot = lax.rem(y + 4 - dy, 4) * 2 + core
            pick = jnp.where(gap == slot * OWN, 1.0, 0.0).astype(jnp.bfloat16)
            total += jnp.dot(pieces[dy][dc], pick, preferred_element_type=jnp.float32)
    whole = total.astype(jnp.bfloat16)
    low[...] = whole[:, :CUT]
    high[...] = whole[:, CUT:]


def lay(at, pieces):
    return pl.pallas_call(
        lay_kernel,
        out_shape=(
            jax.ShapeDtypeStruct((HALF, CUT), jnp.bfloat16),
            jax.ShapeDtypeStruct((HALF, WIDE - CUT), jnp.bfloat16),
        ),
        in_specs=[SMEM] + [VMEM] * 4,
        out_specs=(VMEM, VMEM),
        compiler_params=params(10),
        name="lay",
    )(at, *pieces)


def gather(pieces, left):
    for i in range(len(pieces) // 4):
        own = pieces[4 * i : 4 * i + 4]
        left[i, 0:HALF, 0:CUT] = own[0][...]
        left[i, 0:HALF, CUT:WIDE] = own[1][...]
        left[i, HALF:ROWS, 0:CUT] = own[2][...]
        left[i, HALF:ROWS, CUT:WIDE] = own[3][...]


def product(at, group, native, left, i):
    there, back = group[i]
    source = lax.rem(at[0] + 8 - there + back, 8)
    lanes = pl.ds(pl.multiple_of(source * SPAN // LANES * LANES, LANES), WIDE)
    return lax.dot_general(
        left[i],
        native[:, :, lanes].reshape(A * B, WIDE),
        (((1,), (1,)), ((), ())),
        preferred_element_type=jnp.float32,
    )


def multiply_kernel(group, first, at, *refs):
    n = len(group)
    pieces, native = refs[: 4 * n], refs[4 * n]
    total, left = refs[-2:]
    gather(pieces, left)
    for i in range(n):
        if i == 0 and first:
            total[...] = product(at, group, native, left, i)
        else:
            old = refs[4 * n + 1] if i == 0 else total
            total[...] = old[...] + product(at, group, native, left, i)


def multiply(at, group, pieces, native, old):
    n = len(group)
    first = old is None
    return pl.pallas_call(
        functools.partial(multiply_kernel, group, first),
        out_shape=jax.ShapeDtypeStruct((ROWS, A * B), jnp.float32),
        in_specs=[SMEM] + [VMEM] * (4 * n + 1) + ([] if first else [VMEM]),
        out_specs=VMEM,
        scratch_shapes=[pltpu.VMEM((n, ROWS, WIDE), jnp.bfloat16)],
        input_output_aliases={} if first else {4 * n + 2: 0},
        cost_estimate=pl.CostEstimate(
            flops=2 * n * ROWS * WIDE * B * A, bytes_accessed=n * 1000000, transcendentals=0
        ),
        compiler_params=params(10),
        name="multiply",
    )(at, *map(near, pieces), native, *([] if first else [near(old)]))


CHUNK = 40
CHUNKS = ROWS // CHUNK
SPREAD = APAD // LANES


def last_kernel(group, at, *refs):
    n = len(group)
    pieces, native = refs[: 4 * n], refs[4 * n]
    old, shift, virt, row_term, basis, images, current = refs[4 * n + 1 : 4 * n + 8]
    sigma, parts = refs[4 * n + 8 : 4 * n + 10]
    left, order, spread, sigma_v, out_sems = refs[4 * n + 10 :]
    wide = B * LANES
    come = lax.broadcasted_iota(jnp.int32, (wide, wide), 0)
    goes = lax.broadcasted_iota(jnp.int32, (wide, wide), 1)
    hit = come == lax.rem(goes, LANES) * B + goes // LANES
    order[...] = jnp.where(hit, 1.0, 0.0).astype(jnp.bfloat16)
    gather(pieces, left)
    value = old[...]
    for i in range(n):
        value += product(at, group, native, left, i)
    rounded = value.astype(jnp.bfloat16)
    rounded = jnp.concatenate(
        [rounded, jnp.zeros((ROWS, (APAD - A) * B), jnp.bfloat16)], axis=1
    )
    for t in range(SPREAD):
        run = rounded[:, t * wide : (t + 1) * wide]
        moved = jnp.dot(run, order[...], preferred_element_type=jnp.float32)
        for b in range(B):
            spread[t, pl.ds(b, ROWS, stride=B), :] = moved[:, b * LANES : (b + 1) * LANES]
    core = at[2]
    shifted = shift[0]
    virtual = virt[...]

    def flat(x):
        return x.reshape(CHUNK * B, A).astype(jnp.float32)

    def fold(x):
        return jnp.sum(x.reshape(CHUNK * B // 8, 8, A), axis=0)

    def out_copy(i):
        pairs = pl.ds(pl.multiple_of(i * CHUNK, CHUNK), CHUNK)
        return pltpu.make_async_copy(sigma_v.at[pairs], sigma.at[pairs], out_sems.at[i])

    def body(i, sums):
        pairs = pl.ds(pl.multiple_of(i * CHUNK, CHUNK), CHUNK)
        rows = pl.ds(pl.multiple_of(i * CHUNK * B, CHUNK * B), CHUNK * B)
        from_row = lax.rem(i * CHUNK + HALF * core, ROWS) * B
        taken = pl.ds(pl.multiple_of(from_row, CHUNK * B), CHUNK * B)
        sig = jnp.concatenate([spread[t, taken, :] for t in range(SPREAD)], axis=1)[:, :A]
        sigma_v[pairs] = sig.astype(jnp.bfloat16).reshape(CHUNK, B, A)
        out_copy(i).start()
        inverse = 1.0 / jnp.maximum(virtual + row_term[rows, :], 1.0)
        u = (sig - shifted * flat(current[pairs])) * inverse
        v0 = flat(images[0, pairs]) * inverse
        v1 = flat(images[1, pairs]) * inverse
        new = (
            flat(basis[0, pairs]) * sig,
            flat(basis[1, pairs]) * sig,
            u * u,
            u * v0,
            u * v1,
            v0 * v0,
            v0 * v1,
            v1 * v1,
        )
        return tuple(s + fold(x) for s, x in zip(sums, new))

    zero = jnp.zeros((8, A), jnp.float32)
    sums = lax.fori_loop(0, CHUNKS, body, (zero,) * 8)
    lane = lax.broadcasted_iota(jnp.int32, (1, LANES), 1)
    line = jnp.zeros((1, LANES), jnp.float32)
    for k, s in enumerate(sums):
        line = jnp.where(lane == k, jnp.sum(s, axis=(0, 1), keepdims=True), line)
    parts[...] = jnp.broadcast_to(line[None], (DEVICES, 1, LANES))
    for i in range(CHUNKS):
        out_copy(i).wait()


def last(at, group, pieces, native, old, shift, virt, row_term, basis, images, current):
    n = len(group)
    return pl.pallas_call(
        functools.partial(last_kernel, group),
        out_shape=(
            jax.ShapeDtypeStruct((ROWS, B, A), jnp.bfloat16),
            jax.ShapeDtypeStruct((DEVICES, 1, LANES), jnp.float32),
        ),
        in_specs=[SMEM] + [VMEM] * (4 * n + 2) + [SMEM] + [VMEM] * 5,
        out_specs=(ANY, VMEM),
        scratch_shapes=[
            pltpu.VMEM((n, ROWS, WIDE), jnp.bfloat16),
            pltpu.VMEM((B * LANES, B * LANES), jnp.bfloat16),
            pltpu.VMEM((SPREAD, ROWS * B, LANES), jnp.float32),
            pltpu.VMEM((ROWS, B, A), jnp.bfloat16),
            pltpu.SemaphoreType.DMA((CHUNKS,)),
        ],
        compiler_params=params(14),
        name="last",
    )(at, *map(near, pieces), native, near(old), shift, near(virt), near(row_term), *map(near, (basis, images, current)))


def finish_kernel(gathered, shift, virt, row_term, sigma, current, images, update, flag, update_v, out_sems):
    line = jnp.sum(gathered[...], axis=0)
    lane = lax.broadcasted_iota(jnp.int32, (1, LANES), 1)
    c0, c1, uu, uv0, uv1, v00, v01, v11 = (
        jnp.sum(jnp.where(lane == k, line, 0.0), axis=1, keepdims=True) for k in range(8)
    )
    expanded = uu - 2.0 * (c0 * uv0 + c1 * uv1) + c0 * c0 * v00 + 2.0 * c0 * c1 * v01 + c1 * c1 * v11
    terms = uu + c0 * c0 * v00 + c1 * c1 * v11
    flag[...] = jnp.where(lane == LANES - 1, jnp.where(expanded < 1e-3 * terms, 1.0, 0.0), line)
    scale = lax.rsqrt(jnp.maximum(expanded, 0.0) + 1e-06)
    shifted = shift[0]
    virtual = virt[...]

    def flat(x):
        return x.reshape(CHUNK * B, A).astype(jnp.float32)

    def out_copy(i):
        pairs = pl.ds(pl.multiple_of(i * CHUNK, CHUNK), CHUNK)
        return pltpu.make_async_copy(update_v.at[pairs], update.at[pairs], out_sems.at[i])

    def body(i, nothing):
        pairs = pl.ds(pl.multiple_of(i * CHUNK, CHUNK), CHUNK)
        rows = pl.ds(pl.multiple_of(i * CHUNK * B, CHUNK * B), CHUNK * B)
        resid = flat(sigma[pairs]) - shifted * flat(current[pairs])
        resid = resid - c0 * flat(images[0, pairs]) - c1 * flat(images[1, pairs])
        delta = resid / jnp.maximum(virtual + row_term[rows, :], 1.0)
        update_v[pairs] = (delta * scale).astype(jnp.bfloat16).reshape(CHUNK, B, A)
        out_copy(i).start()
        return nothing

    lax.fori_loop(0, CHUNKS, body, 0)
    for i in range(CHUNKS):
        out_copy(i).wait()


def finish(gathered, shift, virt, row_term, sigma, current, images):
    return pl.pallas_call(
        finish_kernel,
        out_shape=(
            jax.ShapeDtypeStruct((ROWS, B, A), jnp.bfloat16),
            jax.ShapeDtypeStruct((1, LANES), jnp.float32),
        ),
        in_specs=[VMEM, SMEM] + [VMEM] * 5,
        out_specs=(ANY, VMEM),
        scratch_shapes=[pltpu.VMEM((ROWS, B, A), jnp.bfloat16), pltpu.SemaphoreType.DMA((CHUNKS,))],
        compiler_params=params(6),
        name="finish",
    )(near(gathered), shift, *map(near, (virt, row_term, sigma, current, images)))


def ring(n, step):
    return [(i, (i + step) % n) for i in range(n)]


SWAP = [(0, 1), (1, 0)]


def per_device(trial, integrals, basis, images, current, occ_energy, vir_energy, shift):
    x, z, y, c = (lax.axis_index(name) for name in "xzyc")
    mine = lax.dynamic_slice_in_dim(trial, HALF * c, HALF, 0)
    other = lax.dynamic_slice_in_dim(trial, HALF * (1 - c), HALF, 0)
    pair = jnp.stack([mine, lax.ppermute(other, "c", SWAP)])
    pieces = [pair] + [lax.ppermute(pair, "y", ring(4, dy)) for dy in (1, 2, 3)]
    at = jnp.stack([z, y, c]).astype(jnp.int32)
    spans = {(0, 0): lay(at, pieces)}
    for k in (1, 2, 3):
        for there, back, step in ((k, 0, 1), (0, k, -1)):
            before = spans[(max(there - 1, 0), max(back - 1, 0))]
            spans[(there, back)] = tuple(lax.ppermute(s, "z", ring(8, step)) for s in before)
    spans[(4, 0)] = (
        lax.ppermute(spans[(3, 0)][0], "z", ring(8, 1)),
        lax.ppermute(spans[(0, 3)][1], "z", ring(8, -1)),
    )
    native = near(jnp.transpose(integrals, (2, 1, 0)))

    def operands(group):
        arrays = []
        for there, back in group:
            span = spans[(there, back)]
            arrays += list(span) + [lax.ppermute(s, "c", SWAP) for s in span]
        return arrays

    total = None
    for group in GROUPS[:-1]:
        total = multiply(at, group, operands(group), native, total)

    global_row = x * ROWS + jnp.arange(ROWS, dtype=jnp.int32)
    orbitals = jnp.arange(OCCUPIED, dtype=jnp.int32)[None, :]
    first = (global_row // OCCUPIED)[:, None] == orbitals
    second = (global_row % OCCUPIED)[:, None] == orbitals
    pair_energy = jnp.sum(jnp.where(first, occ_energy[None, :], 0.0), axis=1) + jnp.sum(
        jnp.where(second, occ_energy[None, :], 0.0), axis=1
    )
    panel = z * 8 + y * 2 + c
    energy_b = lax.dynamic_slice_in_dim(vir_energy, panel * B, B, 0)
    row_term = (energy_b[None, :] - pair_energy[:, None] - shift[0]).reshape(ROWS * B, 1)
    virt = vir_energy[None, :]
    sigma, parts = last(
        at, GROUPS[-1], operands(GROUPS[-1]), native, total, shift, virt, row_term, basis, images, current
    )
    everyone = ("x", "z", "y", "c")
    gathered = lax.all_to_all(parts, everyone, 0, 0, tiled=True)
    update, line = finish(gathered, shift, virt, row_term, sigma, current, images)
    sums = line[0]

    def direct(_):
        resid = sigma.astype(jnp.float32) - shift[0] * current.astype(jnp.float32)
        for k in range(2):
            resid = resid - sums[k] * images[k].astype(jnp.float32)
        delta = resid / jnp.maximum(virt[None] + row_term.reshape(ROWS, B, 1), 1.0)
        size_sq = lax.psum(jnp.sum(delta * delta), everyone)
        return (0.0, (delta * lax.rsqrt(size_sq + 1e-06)).astype(jnp.bfloat16))

    _, update = lax.while_loop(lambda state: state[0] > 0.5, direct, (sums[LANES - 1], update))
    return (sigma, update, sums[:2])


def solution(mesh):
    fine = Mesh(mesh.devices.reshape(4, 8, 4, 2), ("x", "z", "y", "c"))
    panel = ("z", "y", "c")
    in_specs = (
        P("x", panel),
        P(None, panel, None),
        P(None, "x", panel, None),
        P(None, "x", panel, None),
        P("x", panel, None),
        P(),
        P(),
        P(),
    )
    out_specs = (P("x", panel, None), P("x", panel, None), P())
    return jax.shard_map(
        per_device, mesh=fine, in_specs=in_specs, out_specs=out_specs, check_vma=False
    )
```

```python
import functools

import jax
import jax.numpy as jnp
from jax import lax
from jax.experimental import pallas as pl
from jax.experimental.pallas import tpu as pltpu
from jax.sharding import Mesh, PartitionSpec as P


OCCUPIED = 40
LANES = 128
ROWS = 400
HALF = 200
OWN = 100
SPAN = 800
TILES = 7
WIDE = TILES * LANES
B = 4
A = 300
APAD = 384
DEVICES = 256
GROUPS = (((0, 0),), ((1, 0), (0, 1)), ((2, 0), (0, 2)), ((3, 0), (0, 3)), ((4, 0),))


VMEM = pl.BlockSpec(memory_space=pltpu.VMEM)
SMEM = pl.BlockSpec(memory_space=pltpu.SMEM)
ANY = pl.BlockSpec(memory_space=pl.ANY)


def params(mib):
    return pltpu.CompilerParams(vmem_limit_bytes=mib << 20)


def near(array):
    return pltpu.with_memory_space_constraint(array, pltpu.VMEM)


def lay_kernel(at, *refs):
    pieces, whole = refs[:4], refs[4]
    z, y, c = at[0], at[1], at[2]
    start = lax.rem(z * SPAN, LANES)
    lane = lax.broadcasted_iota(jnp.int32, (OWN, WIDE), 1)
    row = lax.broadcasted_iota(jnp.int32, (OWN, WIDE), 0)
    gap = lane - row - start
    total = jnp.zeros((HALF, WIDE), jnp.float32)
    for dy in range(4):
        for dc in range(2):
            core = c if dc == 0 else 1 - c
            slot = lax.rem(y + 4 - dy, 4) * 2 + core
            pick = jnp.where(gap == slot * OWN, 1.0, 0.0).astype(jnp.bfloat16)
            total += jnp.dot(pieces[dy][dc], pick, preferred_element_type=jnp.float32)
    whole[...] = total.astype(jnp.bfloat16)


def lay(at, pieces):
    return pl.pallas_call(
        lay_kernel,
        out_shape=jax.ShapeDtypeStruct((HALF, WIDE), jnp.bfloat16),
        in_specs=[SMEM] + [VMEM] * 4,
        out_specs=VMEM,
        compiler_params=params(10),
        name="lay",
    )(at, *map(near, pieces))


def gather(pieces, left):
    for i in range(len(pieces) // 2):
        left[i, 0:HALF, :] = pieces[2 * i][...]
        left[i, HALF:ROWS, :] = pieces[2 * i + 1][...]


def part(at, where, native):
    source = lax.rem(at[0] + 8 - where[0] + where[1], 8)
    return native.at[:, :, pl.ds(pl.multiple_of(source * SPAN // LANES * LANES, LANES), WIDE)]


def product(left, right):
    return lax.dot_general(
        left,
        right.reshape(A * B, WIDE),
        (((1,), (1,)), ((), ())),
        preferred_element_type=jnp.float32,
    )


def multiply_kernel(group, first, at, *refs):
    n = len(group)
    pieces, native = refs[: 2 * n], refs[2 * n]
    total, left, right, sems = refs[-4:]
    copies = [
        pltpu.make_async_copy(part(at, group[i], native), right.at[i], sems.at[i]) for i in range(n)
    ]
    for copy in copies:
        copy.start()
    gather(pieces, left)
    for i in range(n):
        copies[i].wait()
        if i == 0 and first:
            total[...] = product(left[i], right[i])
        else:
            old = refs[2 * n + 1] if i == 0 else total
            total[...] = old[...] + product(left[i], right[i])


def multiply(at, group, pieces, native, old):
    n = len(group)
    first = old is None
    return pl.pallas_call(
        functools.partial(multiply_kernel, group, first),
        out_shape=jax.ShapeDtypeStruct((ROWS, A * B), jnp.float32),
        in_specs=[SMEM] + [VMEM] * (2 * n) + [ANY] + ([] if first else [VMEM]),
        out_specs=VMEM,
        scratch_shapes=[
            pltpu.VMEM((n, ROWS, WIDE), jnp.bfloat16),
            pltpu.VMEM((n, A, B, WIDE), jnp.bfloat16),
            pltpu.SemaphoreType.DMA((n,)),
        ],
        input_output_aliases={} if first else {2 * n + 2: 0},
        cost_estimate=pl.CostEstimate(
            flops=2 * n * ROWS * WIDE * B * A, bytes_accessed=n * 3000000, transcendentals=0
        ),
        compiler_params=params(12),
        name="multiply",
    )(at, *map(near, pieces), native, *([] if first else [near(old)]))


CHUNK = 40
CHUNKS = ROWS // CHUNK
SPREAD = APAD // LANES


def fold(x):
    return jnp.sum(x.reshape(CHUNK * B // 8, 8, A), axis=0)


def flat(x):
    return x.reshape(CHUNK * B, A).astype(jnp.float32)


def chunk(i):
    pairs = pl.ds(pl.multiple_of(i * CHUNK, CHUNK), CHUNK)
    rows = pl.ds(pl.multiple_of(i * CHUNK * B, CHUNK * B), CHUNK * B)
    return pairs, rows


def gather_sums(sums, first):
    lane = lax.broadcasted_iota(jnp.int32, (1, LANES), 1)
    line = jnp.zeros((1, LANES), jnp.float32)
    for k, s in enumerate(sums):
        line = jnp.where(lane == first + k, jnp.sum(s, axis=(0, 1), keepdims=True), line)
    return line


def gram_kernel(where, at, virt, row_term, images, native, inverse, line, right, sem):
    copy = pltpu.make_async_copy(part(at, where, native), right, sem)
    copy.start()
    virtual = virt[...]

    def body(i, sums):
        pairs, rows = chunk(i)
        below = 1.0 / jnp.maximum(virtual + row_term[rows, :], 1.0)
        inverse[rows, :] = below
        v0 = flat(images[0, pairs]) * below
        v1 = flat(images[1, pairs]) * below
        return tuple(s + fold(x) for s, x in zip(sums, (v0 * v0, v0 * v1, v1 * v1)))

    zero = jnp.zeros((8, A), jnp.float32)
    line[...] = gather_sums(lax.fori_loop(0, CHUNKS, body, (zero,) * 3), 5)
    copy.wait()


def gram(at, where, virt, row_term, images, native):
    return pl.pallas_call(
        functools.partial(gram_kernel, where),
        out_shape=(
            jax.ShapeDtypeStruct((ROWS * B, A), jnp.float32),
            jax.ShapeDtypeStruct((1, LANES), jnp.float32),
            jax.ShapeDtypeStruct((A, B, WIDE), jnp.bfloat16),
        ),
        in_specs=[SMEM] + [VMEM] * 3 + [ANY],
        out_specs=(VMEM,) * 3,
        scratch_shapes=[pltpu.SemaphoreType.DMA],
        cost_estimate=pl.CostEstimate(flops=20 * ROWS * B * A, bytes_accessed=8000000, transcendentals=0),
        compiler_params=params(2),
        name="gram",
    )(at, *map(near, (virt, row_term, images)), native)


def last_kernel(group, at, *refs):
    n = len(group)
    pieces, right = refs[: 2 * n], refs[2 * n]
    old, shift, inverse, line, basis, images, current = refs[2 * n + 1 : 2 * n + 8]
    sigma, parts = refs[2 * n + 8 : 2 * n + 10]
    left, order, spread, sigma_v, out_sems = refs[2 * n + 10 :]
    wide = B * LANES
    come = lax.broadcasted_iota(jnp.int32, (wide, wide), 0)
    goes = lax.broadcasted_iota(jnp.int32, (wide, wide), 1)
    hit = come == lax.rem(goes, LANES) * B + goes // LANES
    order[...] = jnp.where(hit, 1.0, 0.0).astype(jnp.bfloat16)
    gather(pieces, left)
    rounded = (old[...] + product(left[0], right[...])).astype(jnp.bfloat16)
    rounded = jnp.concatenate(
        [rounded, jnp.zeros((ROWS, (APAD - A) * B), jnp.bfloat16)], axis=1
    )
    for t in range(SPREAD):
        run = rounded[:, t * wide : (t + 1) * wide]
        moved = jnp.dot(run, order[...], preferred_element_type=jnp.float32)
        for b in range(B):
            spread[t, pl.ds(b, ROWS, stride=B), :] = moved[:, b * LANES : (b + 1) * LANES]
    core = at[2]
    shifted = shift[0]

    def out_copy(i):
        pairs, _ = chunk(i)
        return pltpu.make_async_copy(sigma_v.at[pairs], sigma.at[pairs], out_sems.at[i])

    def body(i, sums):
        pairs, rows = chunk(i)
        from_row = lax.rem(i * CHUNK + HALF * core, ROWS) * B
        taken = pl.ds(pl.multiple_of(from_row, CHUNK * B), CHUNK * B)
        sig = jnp.concatenate([spread[t, taken, :] for t in range(SPREAD)], axis=1)[:, :A]
        sigma_v[pairs] = sig.astype(jnp.bfloat16).reshape(CHUNK, B, A)
        out_copy(i).start()
        below = inverse[rows, :]
        u = (sig - shifted * flat(current[pairs])) * below
        w = u * below
        new = (
            flat(basis[0, pairs]) * sig,
            flat(basis[1, pairs]) * sig,
            u * u,
            w * flat(images[0, pairs]),
            w * flat(images[1, pairs]),
        )
        return tuple(s + fold(x) for s, x in zip(sums, new))

    zero = jnp.zeros((8, A), jnp.float32)
    sums = lax.fori_loop(0, CHUNKS, body, (zero,) * 5)
    parts[...] = jnp.broadcast_to((gather_sums(sums, 0) + line[...])[None], (DEVICES, 1, LANES))
    for i in range(CHUNKS):
        out_copy(i).wait()


def last(at, group, pieces, right, old, shift, inverse, line, basis, images, current):
    n = len(group)
    return pl.pallas_call(
        functools.partial(last_kernel, group),
        out_shape=(
            jax.ShapeDtypeStruct((ROWS, B, A), jnp.bfloat16),
            jax.ShapeDtypeStruct((DEVICES, 1, LANES), jnp.float32),
        ),
        in_specs=[SMEM] + [VMEM] * (2 * n + 2) + [SMEM] + [VMEM] * 5,
        out_specs=(ANY, VMEM),
        scratch_shapes=[
            pltpu.VMEM((n, ROWS, WIDE), jnp.bfloat16),
            pltpu.VMEM((B * LANES, B * LANES), jnp.bfloat16),
            pltpu.VMEM((SPREAD, ROWS * B, LANES), jnp.float32),
            pltpu.VMEM((ROWS, B, A), jnp.bfloat16),
            pltpu.SemaphoreType.DMA((CHUNKS,)),
        ],
        compiler_params=params(14),
        name="last",
    )(at, *map(near, pieces), near(right), near(old), shift, *map(near, (inverse, line, basis, images, current)))


def finish_kernel(gathered, shift, inverse, sigma, current, images, update, overlap, flag, update_v, out_sems):
    line = jnp.sum(gathered[...], axis=0)
    lane = lax.broadcasted_iota(jnp.int32, (1, LANES), 1)
    c0, c1, uu, uv0, uv1, v00, v01, v11 = (
        jnp.sum(jnp.where(lane == k, line, 0.0), axis=1, keepdims=True) for k in range(8)
    )
    expanded = uu - 2.0 * (c0 * uv0 + c1 * uv1) + c0 * c0 * v00 + 2.0 * c0 * c1 * v01 + c1 * c1 * v11
    terms = uu + c0 * c0 * v00 + c1 * c1 * v11
    overlap[0] = c0[0, 0]
    overlap[1] = c1[0, 0]
    flag[0] = jnp.where(expanded < 1e-3 * terms, 1.0, 0.0)[0, 0]
    scale = lax.rsqrt(jnp.maximum(expanded, 0.0) + 1e-06)
    shifted = shift[0]

    def out_copy(i):
        pairs, _ = chunk(i)
        return pltpu.make_async_copy(update_v.at[pairs], update.at[pairs], out_sems.at[i])

    def body(i, nothing):
        pairs, rows = chunk(i)
        resid = flat(sigma[pairs]) - shifted * flat(current[pairs])
        resid = resid - c0 * flat(images[0, pairs]) - c1 * flat(images[1, pairs])
        delta = resid * inverse[rows, :]
        update_v[pairs] = (delta * scale).astype(jnp.bfloat16).reshape(CHUNK, B, A)
        out_copy(i).start()
        return nothing

    lax.fori_loop(0, CHUNKS, body, 0)
    for i in range(CHUNKS):
        out_copy(i).wait()


def finish(gathered, shift, inverse, sigma, current, images):
    return pl.pallas_call(
        finish_kernel,
        out_shape=(
            jax.ShapeDtypeStruct((ROWS, B, A), jnp.bfloat16),
            jax.ShapeDtypeStruct((2,), jnp.float32),
            jax.ShapeDtypeStruct((1,), jnp.float32),
        ),
        in_specs=[VMEM, SMEM] + [VMEM] * 4,
        out_specs=(ANY, SMEM, SMEM),
        scratch_shapes=[pltpu.VMEM((ROWS, B, A), jnp.bfloat16), pltpu.SemaphoreType.DMA((CHUNKS,))],
        compiler_params=params(6),
        name="finish",
    )(near(gathered), shift, *map(near, (inverse, sigma, current, images)))


def ring(n, step):
    return [(i, (i + step) % n) for i in range(n)]


SWAP = [(0, 1), (1, 0)]


def per_device(trial, integrals, basis, images, current, occ_energy, vir_energy, shift):
    x, z, y, c = (lax.axis_index(name) for name in "xzyc")
    mine = lax.dynamic_slice_in_dim(trial, HALF * c, HALF, 0)
    other = lax.dynamic_slice_in_dim(trial, HALF * (1 - c), HALF, 0)
    pair = jnp.stack([mine, lax.ppermute(other, "c", SWAP)])
    pieces = [pair] + [lax.ppermute(pair, "y", ring(4, dy)) for dy in (1, 2, 3)]
    at = jnp.stack([z, y, c]).astype(jnp.int32)
    native = pltpu.with_memory_space_constraint(jnp.transpose(integrals, (2, 1, 0)), pltpu.HBM)
    spans = {(0, 0): lay(at, pieces)}
    for k in (1, 2, 3, 4):
        for there, back, step in ((k, 0, 1), (0, k, -1))[: 2 if k < 4 else 1]:
            before = spans[(max(there - 1, 0), max(back - 1, 0))]
            spans[(there, back)] = lax.ppermute(before, "z", ring(8, step))

    def operands(group):
        arrays = []
        for where in group:
            arrays += [spans[where], lax.ppermute(spans[where], "c", SWAP)]
        return arrays

    total = None
    for group in GROUPS[:-1]:
        arrays = operands(group)
        total = multiply(at, group, arrays, native, total)

    global_row = x * ROWS + jnp.arange(ROWS, dtype=jnp.int32)
    orbitals = jnp.arange(OCCUPIED, dtype=jnp.int32)[None, :]
    first = (global_row // OCCUPIED)[:, None] == orbitals
    second = (global_row % OCCUPIED)[:, None] == orbitals
    pair_energy = jnp.sum(jnp.where(first, occ_energy[None, :], 0.0), axis=1) + jnp.sum(
        jnp.where(second, occ_energy[None, :], 0.0), axis=1
    )
    panel = z * 8 + y * 2 + c
    energy_b = lax.dynamic_slice_in_dim(vir_energy, panel * B, B, 0)
    row_term = (energy_b[None, :] - pair_energy[:, None] - shift[0]).reshape(ROWS * B, 1)
    virt = vir_energy[None, :]
    inverse, line, right = gram(at, GROUPS[-1][0], virt, row_term, images, native)
    sigma, parts = last(
        at, GROUPS[-1], operands(GROUPS[-1]), right, total, shift, inverse, line, basis, images, current
    )
    everyone = ("x", "z", "y", "c")
    gathered = lax.all_to_all(parts, everyone, 0, 0, tiled=True)
    update, overlap, flag = finish(gathered, shift, inverse, sigma, current, images)

    def direct(_):
        resid = sigma.astype(jnp.float32) - shift[0] * current.astype(jnp.float32)
        for k in range(2):
            resid = resid - overlap[k] * images[k].astype(jnp.float32)
        delta = resid / jnp.maximum(virt[None] + row_term.reshape(ROWS, B, 1), 1.0)
        size_sq = lax.psum(jnp.sum(delta * delta), everyone)
        return (0.0, (delta * lax.rsqrt(size_sq + 1e-06)).astype(jnp.bfloat16))

    _, update = lax.while_loop(lambda state: state[0] > 0.5, direct, (flag[0], update))
    return (sigma, update, overlap)


def solution(mesh):
    fine = Mesh(mesh.devices.reshape(4, 8, 4, 2), ("x", "z", "y", "c"))
    panel = ("z", "y", "c")
    in_specs = (
        P("x", panel),
        P(None, panel, None),
        P(None, "x", panel, None),
        P(None, "x", panel, None),
        P("x", panel, None),
        P(),
        P(),
        P(),
    )
    out_specs = (P("x", panel, None), P("x", panel, None), P())

    return jax.shard_map(
        per_device, mesh=fine, in_specs=in_specs, out_specs=out_specs, check_vma=False
    )
```

```python
import functools

import jax
import jax.numpy as jnp
from jax import lax
from jax.experimental import pallas as pl
from jax.experimental.pallas import tpu as pltpu
from jax.sharding import Mesh, PartitionSpec as P


OCCUPIED = 40
LANES = 128
ROWS = 400
HALF = 200
OWN = 100
SPAN = 800
TILES = 7
WIDE = TILES * LANES
B = 4
A = 300
APAD = 384
DEVICES = 256
GROUPS = (((0, 0),), ((1, 0), (0, 1)), ((2, 0), (0, 2)), ((3, 0), (0, 3)), ((4, 0),))


VMEM = pl.BlockSpec(memory_space=pltpu.VMEM)
SMEM = pl.BlockSpec(memory_space=pltpu.SMEM)
ANY = pl.BlockSpec(memory_space=pl.ANY)


def params(mib):
    return pltpu.CompilerParams(vmem_limit_bytes=mib << 20)


def near(array):
    return pltpu.with_memory_space_constraint(array, pltpu.VMEM)


def lay_kernel(at, *refs):
    pieces, whole = refs[:4], refs[4]
    z, y, c = at[0], at[1], at[2]
    start = lax.rem(z * SPAN, LANES)
    lane = lax.broadcasted_iota(jnp.int32, (OWN, WIDE), 1)
    row = lax.broadcasted_iota(jnp.int32, (OWN, WIDE), 0)
    gap = lane - row - start
    total = jnp.zeros((HALF, WIDE), jnp.float32)
    for dy in range(4):
        for dc in range(2):
            core = c if dc == 0 else 1 - c
            slot = lax.rem(y + 4 - dy, 4) * 2 + core
            pick = jnp.where(gap == slot * OWN, 1.0, 0.0).astype(jnp.bfloat16)
            total += jnp.dot(pieces[dy][dc], pick, preferred_element_type=jnp.float32)
    whole[...] = total.astype(jnp.bfloat16)


def lay(at, pieces):
    return pl.pallas_call(
        lay_kernel,
        out_shape=jax.ShapeDtypeStruct((HALF, WIDE), jnp.bfloat16),
        in_specs=[SMEM] + [VMEM] * 4,
        out_specs=VMEM,
        compiler_params=params(10),
        name="lay",
    )(at, *map(near, pieces))


def gather(pieces, left):
    for i in range(len(pieces) // 2):
        left[i, 0:HALF, :] = pieces[2 * i][...]
        left[i, HALF:ROWS, :] = pieces[2 * i + 1][...]


def part(at, where, native):
    source = lax.rem(at[0] + 8 - where[0] + where[1], 8)
    return native.at[:, :, pl.ds(pl.multiple_of(source * SPAN // LANES * LANES, LANES), WIDE)]


def product(left, right):
    return lax.dot_general(
        left,
        right.reshape(A * B, WIDE),
        (((1,), (1,)), ((), ())),
        preferred_element_type=jnp.float32,
    )


def fetch(at, group, native, right, sems):
    copies = [
        pltpu.make_async_copy(part(at, where, native), right.at[i], sems.at[i])
        for i, where in enumerate(group)
    ]
    for copy in copies:
        copy.start()
    return copies


def parts_of(group):
    return jax.ShapeDtypeStruct((len(group), A, B, WIDE), jnp.bfloat16)


def multiply_kernel(group, following, first, at, *refs):
    n = len(group)
    pieces, native, right = refs[: 2 * n], refs[2 * n], refs[2 * n + 1]
    total, ahead, left, sems = refs[-4:]
    copies = fetch(at, following, native, ahead, sems)
    gather(pieces, left)
    for i in range(n):
        if i == 0 and first:
            total[...] = product(left[i], right[i])
        else:
            old = refs[2 * n + 2] if i == 0 else total
            total[...] = old[...] + product(left[i], right[i])
    for copy in copies:
        copy.wait()


def multiply(at, group, following, pieces, native, right, old):
    n = len(group)
    first = old is None
    return pl.pallas_call(
        functools.partial(multiply_kernel, group, following, first),
        out_shape=(jax.ShapeDtypeStruct((ROWS, A * B), jnp.float32), parts_of(following)),
        in_specs=[SMEM] + [VMEM] * (2 * n) + [ANY, VMEM] + ([] if first else [VMEM]),
        out_specs=(VMEM, VMEM),
        scratch_shapes=[
            pltpu.VMEM((n, ROWS, WIDE), jnp.bfloat16),
            pltpu.SemaphoreType.DMA((len(following),)),
        ],
        input_output_aliases={} if first else {2 * n + 3: 0},
        cost_estimate=pl.CostEstimate(
            flops=2 * n * ROWS * WIDE * B * A, bytes_accessed=n * 3000000, transcendentals=0
        ),
        compiler_params=params(8),
        name="multiply",
    )(at, *map(near, pieces), native, near(right), *([] if first else [near(old)]))


CHUNK = 40
CHUNKS = ROWS // CHUNK
SPREAD = APAD // LANES


def fold(x):
    return jnp.sum(x.reshape(CHUNK * B // 8, 8, A), axis=0)


def flat(x):
    return x.reshape(CHUNK * B, A).astype(jnp.float32)


def chunk(i):
    pairs = pl.ds(pl.multiple_of(i * CHUNK, CHUNK), CHUNK)
    rows = pl.ds(pl.multiple_of(i * CHUNK * B, CHUNK * B), CHUNK * B)
    return pairs, rows


def gather_sums(sums, first):
    lane = lax.broadcasted_iota(jnp.int32, (1, LANES), 1)
    line = jnp.zeros((1, LANES), jnp.float32)
    for k, s in enumerate(sums):
        line = jnp.where(lane == first + k, jnp.sum(s, axis=(0, 1), keepdims=True), line)
    return line


def gram_kernel(group, at, virt, row_term, images, native, inverse, line, ahead, sems):
    copies = fetch(at, group, native, ahead, sems)
    virtual = virt[...]

    def body(i, sums):
        pairs, rows = chunk(i)
        below = 1.0 / jnp.maximum(virtual + row_term[rows, :], 1.0)
        inverse[rows, :] = below
        v0 = flat(images[0, pairs]) * below
        v1 = flat(images[1, pairs]) * below
        return tuple(s + fold(x) for s, x in zip(sums, (v0 * v0, v0 * v1, v1 * v1)))

    zero = jnp.zeros((8, A), jnp.float32)
    line[...] = gather_sums(lax.fori_loop(0, CHUNKS, body, (zero,) * 3), 5)
    for copy in copies:
        copy.wait()


def gram(at, group, virt, row_term, images, native):
    return pl.pallas_call(
        functools.partial(gram_kernel, group),
        out_shape=(
            jax.ShapeDtypeStruct((ROWS * B, A), jnp.float32),
            jax.ShapeDtypeStruct((1, LANES), jnp.float32),
            parts_of(group),
        ),
        in_specs=[SMEM] + [VMEM] * 3 + [ANY],
        out_specs=(VMEM,) * 3,
        scratch_shapes=[pltpu.SemaphoreType.DMA((len(group),))],
        cost_estimate=pl.CostEstimate(flops=20 * ROWS * B * A, bytes_accessed=8000000, transcendentals=0),
        compiler_params=params(2),
        name="gram",
    )(at, *map(near, (virt, row_term, images)), native)


def last_kernel(group, at, *refs):
    n = len(group)
    pieces, right = refs[: 2 * n], refs[2 * n]
    old, shift, inverse, line, basis, images, current = refs[2 * n + 1 : 2 * n + 8]
    sigma, parts = refs[2 * n + 8 : 2 * n + 10]
    left, order, spread, sigma_v, out_sems = refs[2 * n + 10 :]
    wide = B * LANES
    come = lax.broadcasted_iota(jnp.int32, (wide, wide), 0)
    goes = lax.broadcasted_iota(jnp.int32, (wide, wide), 1)
    hit = come == lax.rem(goes, LANES) * B + goes // LANES
    order[...] = jnp.where(hit, 1.0, 0.0).astype(jnp.bfloat16)
    gather(pieces, left)
    rounded = (old[...] + product(left[0], right[0])).astype(jnp.bfloat16)
    rounded = jnp.concatenate(
        [rounded, jnp.zeros((ROWS, (APAD - A) * B), jnp.bfloat16)], axis=1
    )
    for t in range(SPREAD):
        run = rounded[:, t * wide : (t + 1) * wide]
        moved = jnp.dot(run, order[...], preferred_element_type=jnp.float32)
        for b in range(B):
            spread[t, pl.ds(b, ROWS, stride=B), :] = moved[:, b * LANES : (b + 1) * LANES]
    core = at[2]
    shifted = shift[0]

    def out_copy(i):
        pairs, _ = chunk(i)
        return pltpu.make_async_copy(sigma_v.at[pairs], sigma.at[pairs], out_sems.at[i])

    def body(i, sums):
        pairs, rows = chunk(i)
        from_row = lax.rem(i * CHUNK + HALF * core, ROWS) * B
        taken = pl.ds(pl.multiple_of(from_row, CHUNK * B), CHUNK * B)
        sig = jnp.concatenate([spread[t, taken, :] for t in range(SPREAD)], axis=1)[:, :A]
        sigma_v[pairs] = sig.astype(jnp.bfloat16).reshape(CHUNK, B, A)
        out_copy(i).start()
        below = inverse[rows, :]
        u = (sig - shifted * flat(current[pairs])) * below
        w = u * below
        new = (
            flat(basis[0, pairs]) * sig,
            flat(basis[1, pairs]) * sig,
            u * u,
            w * flat(images[0, pairs]),
            w * flat(images[1, pairs]),
        )
        return tuple(s + fold(x) for s, x in zip(sums, new))

    zero = jnp.zeros((8, A), jnp.float32)
    sums = lax.fori_loop(0, CHUNKS, body, (zero,) * 5)
    parts[...] = jnp.broadcast_to((gather_sums(sums, 0) + line[...])[None], (DEVICES, 1, LANES))
    for i in range(CHUNKS):
        out_copy(i).wait()


def last(at, group, pieces, right, old, shift, inverse, line, basis, images, current):
    n = len(group)
    return pl.pallas_call(
        functools.partial(last_kernel, group),
        out_shape=(
            jax.ShapeDtypeStruct((ROWS, B, A), jnp.bfloat16),
            jax.ShapeDtypeStruct((DEVICES, 1, LANES), jnp.float32),
        ),
        in_specs=[SMEM] + [VMEM] * (2 * n + 2) + [SMEM] + [VMEM] * 5,
        out_specs=(ANY, VMEM),
        scratch_shapes=[
            pltpu.VMEM((n, ROWS, WIDE), jnp.bfloat16),
            pltpu.VMEM((B * LANES, B * LANES), jnp.bfloat16),
            pltpu.VMEM((SPREAD, ROWS * B, LANES), jnp.float32),
            pltpu.VMEM((ROWS, B, A), jnp.bfloat16),
            pltpu.SemaphoreType.DMA((CHUNKS,)),
        ],
        compiler_params=params(14),
        name="last",
    )(at, *map(near, pieces), near(right), near(old), shift, *map(near, (inverse, line, basis, images, current)))


def finish_kernel(gathered, shift, inverse, sigma, current, images, update, overlap, flag, update_v, out_sems):
    line = jnp.sum(gathered[...], axis=0)
    lane = lax.broadcasted_iota(jnp.int32, (1, LANES), 1)
    c0, c1, uu, uv0, uv1, v00, v01, v11 = (
        jnp.sum(jnp.where(lane == k, line, 0.0), axis=1, keepdims=True) for k in range(8)
    )
    expanded = uu - 2.0 * (c0 * uv0 + c1 * uv1) + c0 * c0 * v00 + 2.0 * c0 * c1 * v01 + c1 * c1 * v11
    terms = uu + c0 * c0 * v00 + c1 * c1 * v11
    overlap[0] = c0[0, 0]
    overlap[1] = c1[0, 0]
    flag[0] = jnp.where(expanded < 1e-3 * terms, 1.0, 0.0)[0, 0]
    scale = lax.rsqrt(jnp.maximum(expanded, 0.0) + 1e-06)
    shifted = shift[0]

    def out_copy(i):
        pairs, _ = chunk(i)
        return pltpu.make_async_copy(update_v.at[pairs], update.at[pairs], out_sems.at[i])

    def body(i, nothing):
        pairs, rows = chunk(i)
        resid = flat(sigma[pairs]) - shifted * flat(current[pairs])
        resid = resid - c0 * flat(images[0, pairs]) - c1 * flat(images[1, pairs])
        delta = resid * inverse[rows, :]
        update_v[pairs] = (delta * scale).astype(jnp.bfloat16).reshape(CHUNK, B, A)
        out_copy(i).start()
        return nothing

    lax.fori_loop(0, CHUNKS, body, 0)
    for i in range(CHUNKS):
        out_copy(i).wait()


def finish(gathered, shift, inverse, sigma, current, images):
    return pl.pallas_call(
        finish_kernel,
        out_shape=(
            jax.ShapeDtypeStruct((ROWS, B, A), jnp.bfloat16),
            jax.ShapeDtypeStruct((2,), jnp.float32),
            jax.ShapeDtypeStruct((1,), jnp.float32),
        ),
        in_specs=[VMEM, SMEM] + [VMEM] * 4,
        out_specs=(ANY, SMEM, SMEM),
        scratch_shapes=[pltpu.VMEM((ROWS, B, A), jnp.bfloat16), pltpu.SemaphoreType.DMA((CHUNKS,))],
        compiler_params=params(6),
        name="finish",
    )(near(gathered), shift, *map(near, (inverse, sigma, current, images)))


def ring(n, step):
    return [(i, (i + step) % n) for i in range(n)]


SWAP = [(0, 1), (1, 0)]


def per_device(trial, integrals, basis, images, current, occ_energy, vir_energy, shift):
    x, z, y, c = (lax.axis_index(name) for name in "xzyc")
    mine = lax.dynamic_slice_in_dim(trial, HALF * c, HALF, 0)
    other = lax.dynamic_slice_in_dim(trial, HALF * (1 - c), HALF, 0)
    pair = jnp.stack([mine, lax.ppermute(other, "c", SWAP)])
    pieces = [pair] + [lax.ppermute(pair, "y", ring(4, dy)) for dy in (1, 2, 3)]
    at = jnp.stack([z, y, c]).astype(jnp.int32)
    native = pltpu.with_memory_space_constraint(jnp.transpose(integrals, (2, 1, 0)), pltpu.HBM)
    spans = {(0, 0): lay(at, pieces)}
    for k in (1, 2, 3, 4):
        for there, back, step in ((k, 0, 1), (0, k, -1))[: 2 if k < 4 else 1]:
            before = spans[(max(there - 1, 0), max(back - 1, 0))]
            spans[(there, back)] = lax.ppermute(before, "z", ring(8, step))

    def operands(group):
        arrays = []
        for where in group:
            arrays += [spans[where], lax.ppermute(spans[where], "c", SWAP)]
        return arrays

    global_row = x * ROWS + jnp.arange(ROWS, dtype=jnp.int32)
    orbitals = jnp.arange(OCCUPIED, dtype=jnp.int32)[None, :]
    first = (global_row // OCCUPIED)[:, None] == orbitals
    second = (global_row % OCCUPIED)[:, None] == orbitals
    pair_energy = jnp.sum(jnp.where(first, occ_energy[None, :], 0.0), axis=1) + jnp.sum(
        jnp.where(second, occ_energy[None, :], 0.0), axis=1
    )
    panel = z * 8 + y * 2 + c
    energy_b = lax.dynamic_slice_in_dim(vir_energy, panel * B, B, 0)
    row_term = (energy_b[None, :] - pair_energy[:, None] - shift[0]).reshape(ROWS * B, 1)
    virt = vir_energy[None, :]
    inverse, line, right = gram(at, GROUPS[0], virt, row_term, images, native)
    total = None
    for k, group in enumerate(GROUPS[:-1]):
        arrays = operands(group)
        total, right = multiply(at, group, GROUPS[k + 1], arrays, native, right, total)
    sigma, parts = last(
        at, GROUPS[-1], operands(GROUPS[-1]), right, total, shift, inverse, line, basis, images, current
    )
    everyone = ("x", "z", "y", "c")
    gathered = lax.all_to_all(parts, everyone, 0, 0, tiled=True)
    update, overlap, flag = finish(gathered, shift, inverse, sigma, current, images)

    def direct(_):
        resid = sigma.astype(jnp.float32) - shift[0] * current.astype(jnp.float32)
        for k in range(2):
            resid = resid - overlap[k] * images[k].astype(jnp.float32)
        delta = resid / jnp.maximum(virt[None] + row_term.reshape(ROWS, B, 1), 1.0)
        size_sq = lax.psum(jnp.sum(delta * delta), everyone)
        return (0.0, (delta * lax.rsqrt(size_sq + 1e-06)).astype(jnp.bfloat16))

    _, update = lax.while_loop(lambda state: state[0] > 0.5, direct, (flag[0], update))
    return (sigma, update, overlap)


def solution(mesh):
    fine = Mesh(mesh.devices.reshape(4, 8, 4, 2), ("x", "z", "y", "c"))
    panel = ("z", "y", "c")
    in_specs = (
        P("x", panel),
        P(None, panel, None),
        P(None, "x", panel, None),
        P(None, "x", panel, None),
        P("x", panel, None),
        P(),
        P(),
        P(),
    )
    out_specs = (P("x", panel, None), P("x", panel, None), P())

    return jax.shard_map(
        per_device, mesh=fine, in_specs=in_specs, out_specs=out_specs, check_vma=False
    )
```

```python
import functools

import jax
import jax.numpy as jnp
from jax import lax
from jax.experimental import pallas as pl
from jax.experimental.pallas import tpu as pltpu
from jax.sharding import Mesh, PartitionSpec as P


OCCUPIED = 40
LANES = 128
ROWS = 400
HALF = 200
OWN = 100
SPAN = 800
TILES = 7
WIDE = TILES * LANES
B = 4
A = 300
APAD = 384
DEVICES = 256
SUMS = 8
GROUPS = (((0, 0),), ((1, 0), (0, 1)), ((2, 0), (0, 2)), ((3, 0), (0, 3)), ((4, 0),))


VMEM = pl.BlockSpec(memory_space=pltpu.VMEM)
SMEM = pl.BlockSpec(memory_space=pltpu.SMEM)
ANY = pl.BlockSpec(memory_space=pl.ANY)


def params(mib):
    return pltpu.CompilerParams(vmem_limit_bytes=mib << 20)


def near(array):
    return pltpu.with_memory_space_constraint(array, pltpu.VMEM)


def picks_kernel(at, picks, order):
    z, y, c = at[0], at[1], at[2]
    start = lax.rem(z * SPAN, LANES)
    lane = lax.broadcasted_iota(jnp.int32, (OWN, WIDE), 1)
    row = lax.broadcasted_iota(jnp.int32, (OWN, WIDE), 0)
    gap = lane - row - start
    for dy in range(4):
        for dc in range(2):
            core = c if dc == 0 else 1 - c
            slot = lax.rem(y + 4 - dy, 4) * 2 + core
            picks[dy, dc] = jnp.where(gap == slot * OWN, 1.0, 0.0).astype(jnp.bfloat16)
    wide = B * LANES
    come = lax.broadcasted_iota(jnp.int32, (wide, wide), 0)
    goes = lax.broadcasted_iota(jnp.int32, (wide, wide), 1)
    hit = come == lax.rem(goes, LANES) * B + goes // LANES
    order[...] = jnp.where(hit, 1.0, 0.0).astype(jnp.bfloat16)


def make_picks(at):
    return pl.pallas_call(
        picks_kernel,
        out_shape=(
            jax.ShapeDtypeStruct((4, 2, OWN, WIDE), jnp.bfloat16),
            jax.ShapeDtypeStruct((B * LANES, B * LANES), jnp.bfloat16),
        ),
        in_specs=[SMEM],
        out_specs=(VMEM, VMEM),
        compiler_params=params(4),
        name="picks",
    )(at)


def lay_kernel(*refs):
    pieces, picks, whole = refs[:4], refs[4], refs[-1]
    total = jnp.zeros((HALF, WIDE), jnp.float32)
    for dy in range(4):
        for dc in range(2):
            total += jnp.dot(pieces[dy][dc], picks[dy, dc], preferred_element_type=jnp.float32)
    whole[...] = total.astype(jnp.bfloat16)


def lay(pieces, picks, *early):
    return pl.pallas_call(
        lay_kernel,
        out_shape=jax.ShapeDtypeStruct((HALF, WIDE), jnp.bfloat16),
        in_specs=[VMEM] * (5 + len(early)),
        out_specs=VMEM,
        compiler_params=params(4),
        name="lay",
    )(*map(near, (*pieces, picks, *early)))


def gather(pieces, left):
    for i in range(len(pieces) // 2):
        left[i, 0:HALF, :] = pieces[2 * i][...]
        left[i, HALF:ROWS, :] = pieces[2 * i + 1][...]


def part(at, where, native):
    source = lax.rem(at[0] + 8 - where[0] + where[1], 8)
    return native.at[:, :, pl.ds(pl.multiple_of(source * SPAN // LANES * LANES, LANES), WIDE)]


def product(left, right):
    return lax.dot_general(
        left,
        right.reshape(A * B, WIDE),
        (((1,), (1,)), ((), ())),
        preferred_element_type=jnp.float32,
    )


def fetch(at, group, native, right, sems):
    copies = [
        pltpu.make_async_copy(part(at, where, native), right.at[i], sems.at[i])
        for i, where in enumerate(group)
    ]
    for copy in copies:
        copy.start()
    return copies


def parts_of(group):
    return jax.ShapeDtypeStruct((len(group), A, B, WIDE), jnp.bfloat16)


def multiply_kernel(group, following, first, at, *refs):
    n = len(group)
    pieces, native, right = refs[: 2 * n], refs[2 * n], refs[2 * n + 1]
    total, ahead, left, sems = refs[-4:]
    copies = fetch(at, following, native, ahead, sems)
    gather(pieces, left)
    for i in range(n):
        if i == 0 and first:
            total[...] = product(left[i], right[i])
        else:
            old = refs[2 * n + 2] if i == 0 else total
            total[...] = old[...] + product(left[i], right[i])
    for copy in copies:
        copy.wait()


def multiply(at, group, following, pieces, native, right, old):
    n = len(group)
    first = old is None
    return pl.pallas_call(
        functools.partial(multiply_kernel, group, following, first),
        out_shape=(jax.ShapeDtypeStruct((ROWS, A * B), jnp.float32), parts_of(following)),
        in_specs=[SMEM] + [VMEM] * (2 * n) + [ANY, VMEM] + ([] if first else [VMEM]),
        out_specs=(VMEM, VMEM),
        scratch_shapes=[
            pltpu.VMEM((n, ROWS, WIDE), jnp.bfloat16),
            pltpu.SemaphoreType.DMA((len(following),)),
        ],
        input_output_aliases={} if first else {2 * n + 3: 0},
        cost_estimate=pl.CostEstimate(
            flops=2 * n * ROWS * WIDE * B * A, bytes_accessed=n * 3000000, transcendentals=0
        ),
        compiler_params=params(8),
        name="multiply",
    )(at, *map(near, pieces), native, near(right), *([] if first else [near(old)]))


CHUNK = 40
CHUNKS = ROWS // CHUNK
SPREAD = APAD // LANES


def fold(x):
    return jnp.sum(x.reshape(CHUNK * B // 8, 8, A), axis=0)


def flat(x):
    return x.reshape(CHUNK * B, A).astype(jnp.float32)


def chunk(i):
    pairs = pl.ds(pl.multiple_of(i * CHUNK, CHUNK), CHUNK)
    rows = pl.ds(pl.multiple_of(i * CHUNK * B, CHUNK * B), CHUNK * B)
    return pairs, rows


def gather_sums(sums, first):
    lane = lax.broadcasted_iota(jnp.int32, (1, LANES), 1)
    line = jnp.zeros((1, LANES), jnp.float32)
    for k, s in enumerate(sums):
        line = jnp.where(lane == first + k, jnp.sum(s, axis=(0, 1), keepdims=True), line)
    return line


def gram_kernel(group, at, virt, row_term, images, native, inverse, line, ahead, sems):
    copies = fetch(at, group, native, ahead, sems)
    virtual = virt[...]

    def body(i, sums):
        pairs, rows = chunk(i)
        below = 1.0 / jnp.maximum(virtual + row_term[rows, :], 1.0)
        inverse[rows, :] = below
        v0 = flat(images[0, pairs]) * below
        v1 = flat(images[1, pairs]) * below
        return tuple(s + fold(x) for s, x in zip(sums, (v0 * v0, v0 * v1, v1 * v1)))

    zero = jnp.zeros((8, A), jnp.float32)
    line[...] = gather_sums(lax.fori_loop(0, CHUNKS, body, (zero,) * 3), 5)
    for copy in copies:
        copy.wait()


def gram(at, group, virt, row_term, images, native):
    return pl.pallas_call(
        functools.partial(gram_kernel, group),
        out_shape=(
            jax.ShapeDtypeStruct((ROWS * B, A), jnp.float32),
            jax.ShapeDtypeStruct((1, LANES), jnp.float32),
            parts_of(group),
        ),
        in_specs=[SMEM] + [VMEM] * 3 + [ANY],
        out_specs=(VMEM,) * 3,
        scratch_shapes=[pltpu.SemaphoreType.DMA((len(group),))],
        cost_estimate=pl.CostEstimate(flops=20 * ROWS * B * A, bytes_accessed=8000000, transcendentals=0),
        compiler_params=params(2),
        name="gram",
    )(at, *map(near, (virt, row_term, images)), native)


def last_kernel(group, at, *refs):
    n = len(group)
    pieces, right = refs[: 2 * n], refs[2 * n]
    old, shift, order, inverse, line, basis, images, current = refs[2 * n + 1 : 2 * n + 9]
    sigma, parts = refs[2 * n + 9 : 2 * n + 11]
    left, spread, sigma_v, out_sems = refs[2 * n + 11 :]
    wide = B * LANES
    gather(pieces, left)
    rounded = (old[...] + product(left[0], right[0])).astype(jnp.bfloat16)
    rounded = jnp.concatenate(
        [rounded, jnp.zeros((ROWS, (APAD - A) * B), jnp.bfloat16)], axis=1
    )
    for t in range(SPREAD):
        run = rounded[:, t * wide : (t + 1) * wide]
        moved = jnp.dot(run, order[...], preferred_element_type=jnp.float32)
        for b in range(B):
            spread[t, pl.ds(b, ROWS, stride=B), :] = moved[:, b * LANES : (b + 1) * LANES]
    core = at[2]
    shifted = shift[0]

    def out_copy(i):
        pairs, _ = chunk(i)
        return pltpu.make_async_copy(sigma_v.at[pairs], sigma.at[pairs], out_sems.at[i])

    def body(i, sums):
        pairs, rows = chunk(i)
        from_row = lax.rem(i * CHUNK + HALF * core, ROWS) * B
        taken = pl.ds(pl.multiple_of(from_row, CHUNK * B), CHUNK * B)
        sig = jnp.concatenate([spread[t, taken, :] for t in range(SPREAD)], axis=1)[:, :A]
        sigma_v[pairs] = sig.astype(jnp.bfloat16).reshape(CHUNK, B, A)
        out_copy(i).start()
        below = inverse[rows, :]
        u = (sig - shifted * flat(current[pairs])) * below
        w = u * below
        new = (
            flat(basis[0, pairs]) * sig,
            flat(basis[1, pairs]) * sig,
            u * u,
            w * flat(images[0, pairs]),
            w * flat(images[1, pairs]),
        )
        return tuple(s + fold(x) for s, x in zip(sums, new))

    zero = jnp.zeros((8, A), jnp.float32)
    sums = lax.fori_loop(0, CHUNKS, body, (zero,) * 5)
    parts[...] = jnp.broadcast_to((gather_sums(sums, 0) + line[...])[None, :, :SUMS], (DEVICES, 1, SUMS))
    for i in range(CHUNKS):
        out_copy(i).wait()


def last(at, group, pieces, right, old, shift, order, inverse, line, basis, images, current):
    n = len(group)
    return pl.pallas_call(
        functools.partial(last_kernel, group),
        out_shape=(
            jax.ShapeDtypeStruct((ROWS, B, A), jnp.bfloat16),
            jax.ShapeDtypeStruct((DEVICES, 1, SUMS), jnp.float32),
        ),
        in_specs=[SMEM] + [VMEM] * (2 * n + 2) + [SMEM] + [VMEM] * 6,
        out_specs=(ANY, VMEM),
        scratch_shapes=[
            pltpu.VMEM((n, ROWS, WIDE), jnp.bfloat16),
            pltpu.VMEM((SPREAD, ROWS * B, LANES), jnp.float32),
            pltpu.VMEM((ROWS, B, A), jnp.bfloat16),
            pltpu.SemaphoreType.DMA((CHUNKS,)),
        ],
        compiler_params=params(14),
        name="last",
    )(at, *map(near, pieces), near(right), near(old), shift, *map(near, (order, inverse, line, basis, images, current)))


def finish_kernel(gathered, shift, inverse, sigma, current, images, update, overlap, flag, update_v, out_sems):
    line = jnp.sum(gathered[...], axis=0)
    lane = lax.broadcasted_iota(jnp.int32, (1, SUMS), 1)
    c0, c1, uu, uv0, uv1, v00, v01, v11 = (
        jnp.sum(jnp.where(lane == k, line, 0.0), axis=1, keepdims=True) for k in range(8)
    )
    expanded = uu - 2.0 * (c0 * uv0 + c1 * uv1) + c0 * c0 * v00 + 2.0 * c0 * c1 * v01 + c1 * c1 * v11
    terms = uu + c0 * c0 * v00 + c1 * c1 * v11
    overlap[0] = c0[0, 0]
    overlap[1] = c1[0, 0]
    flag[0] = jnp.where(expanded < 1e-3 * terms, 1.0, 0.0)[0, 0]
    scale = lax.rsqrt(jnp.maximum(expanded, 0.0) + 1e-06)
    shifted = shift[0]

    def out_copy(i):
        pairs, _ = chunk(i)
        return pltpu.make_async_copy(update_v.at[pairs], update.at[pairs], out_sems.at[i])

    def body(i, nothing):
        pairs, rows = chunk(i)
        resid = flat(sigma[pairs]) - shifted * flat(current[pairs])
        resid = resid - c0 * flat(images[0, pairs]) - c1 * flat(images[1, pairs])
        delta = resid * inverse[rows, :]
        update_v[pairs] = (delta * scale).astype(jnp.bfloat16).reshape(CHUNK, B, A)
        out_copy(i).start()
        return nothing

    lax.fori_loop(0, CHUNKS, body, 0)
    for i in range(CHUNKS):
        out_copy(i).wait()


def finish(gathered, shift, inverse, sigma, current, images):
    return pl.pallas_call(
        finish_kernel,
        out_shape=(
            jax.ShapeDtypeStruct((ROWS, B, A), jnp.bfloat16),
            jax.ShapeDtypeStruct((2,), jnp.float32),
            jax.ShapeDtypeStruct((1,), jnp.float32),
        ),
        in_specs=[VMEM, SMEM] + [VMEM] * 4,
        out_specs=(ANY, SMEM, SMEM),
        scratch_shapes=[pltpu.VMEM((ROWS, B, A), jnp.bfloat16), pltpu.SemaphoreType.DMA((CHUNKS,))],
        compiler_params=params(6),
        name="finish",
    )(near(gathered), shift, *map(near, (inverse, sigma, current, images)))


def ring(n, step):
    return [(i, (i + step) % n) for i in range(n)]


SWAP = [(0, 1), (1, 0)]


def per_device(trial, integrals, basis, images, current, occ_energy, vir_energy, shift):
    x, z, y, c = (lax.axis_index(name) for name in "xzyc")
    mine = lax.dynamic_slice_in_dim(trial, HALF * c, HALF, 0)
    other = lax.dynamic_slice_in_dim(trial, HALF * (1 - c), HALF, 0)
    pair = jnp.stack([mine, lax.ppermute(other, "c", SWAP)])
    at = jnp.stack([z, y, c]).astype(jnp.int32)
    pair, at, occ_energy, early_vir = lax.optimization_barrier((pair, at, occ_energy, vir_energy))
    pieces = [pair] + [lax.ppermute(pair, "y", ring(4, dy)) for dy in (1, 2, 3)]
    native = pltpu.with_memory_space_constraint(jnp.transpose(integrals, (2, 1, 0)), pltpu.HBM)
    global_row = x * ROWS + jnp.arange(ROWS, dtype=jnp.int32)
    orbitals = jnp.arange(OCCUPIED, dtype=jnp.int32)[None, :]
    first = (global_row // OCCUPIED)[:, None] == orbitals
    second = (global_row % OCCUPIED)[:, None] == orbitals
    pair_energy = jnp.sum(jnp.where(first, occ_energy[None, :], 0.0), axis=1) + jnp.sum(
        jnp.where(second, occ_energy[None, :], 0.0), axis=1
    )
    panel = z * 8 + y * 2 + c
    energy_b = lax.dynamic_slice_in_dim(early_vir, panel * B, B, 0)
    row_term = (energy_b[None, :] - pair_energy[:, None] - shift[0]).reshape(ROWS * B, 1)
    virt = early_vir[None, :]
    picks, order = make_picks(at)
    spans = {(0, 0): lay(pieces, picks, virt, row_term)}
    for k in (1, 2, 3, 4):
        for there, back, step in ((k, 0, 1), (0, k, -1))[: 2 if k < 4 else 1]:
            before = spans[(max(there - 1, 0), max(back - 1, 0))]
            spans[(there, back)] = lax.ppermute(before, "z", ring(8, step))

    def operands(group):
        arrays = []
        for there, back in group:
            span = spans[(there, back)]
            arrays += [span, lax.ppermute(span, "c", SWAP)]
        return arrays

    inverse, line, right = gram(at, GROUPS[0], virt, row_term, images, native)
    total = None
    for k, group in enumerate(GROUPS[:-1]):
        arrays = operands(group)
        total, right = multiply(at, group, GROUPS[k + 1], arrays, native, right, total)
    sigma, parts = last(
        at, GROUPS[-1], operands(GROUPS[-1]), right, total, shift, order, inverse, line, basis, images, current
    )
    everyone = ("x", "z", "y", "c")
    gathered = lax.all_to_all(parts, everyone, 0, 0, tiled=True)
    update, overlap, flag = finish(gathered, shift, inverse, sigma, current, images)

    def direct(_):
        resid = sigma.astype(jnp.float32) - shift[0] * current.astype(jnp.float32)
        for k in range(2):
            resid = resid - overlap[k] * images[k].astype(jnp.float32)
        delta = resid / jnp.maximum(virt[None] + row_term.reshape(ROWS, B, 1), 1.0)
        size_sq = lax.psum(jnp.sum(delta * delta), everyone)
        return (0.0, (delta * lax.rsqrt(size_sq + 1e-06)).astype(jnp.bfloat16))

    _, update = lax.while_loop(lambda state: state[0] > 0.5, direct, (flag[0], update))
    return (sigma, update, overlap)


def solution(mesh):
    fine = Mesh(mesh.devices.reshape(4, 8, 4, 2), ("x", "z", "y", "c"))
    panel = ("z", "y", "c")
    in_specs = (
        P("x", panel),
        P(None, panel, None),
        P(None, "x", panel, None),
        P(None, "x", panel, None),
        P("x", panel, None),
        P(),
        P(),
        P(),
    )
    out_specs = (P("x", panel, None), P("x", panel, None), P())

    return jax.shard_map(
        per_device, mesh=fine, in_specs=in_specs, out_specs=out_specs, check_vma=False
    )
```
